128 devices in a mesh: gy: 32 (over y, x, z_hi), gz: 4 (over z_lo, core).
Axes of the slice: x: 4, y: 4, z: 4 (z_hi: 2, z_lo: 2; z = z_hi * 2 + z_lo), core: 2. Of those that a mesh axis runs over, the one named last changes fastest.
Arguments:
- codes: int32 [1536, 96, 256], P('gy', 'gz'), may hold values from 0 to 15, as said below
- cell_volume: float32 [1536, 96, 256], P('gy', 'gz'), may hold values from 0.25 to 4
Outputs:
- entropy: float32 [1536, 96, 256], P('gy', 'gz')
The draws below stay inside these ranges and needn't reach their ends.
Inputs may be any that keep to these rules, and one draw needn't show every extreme that they name: The bin codes form regions of a few cells, each region with its own mixture of codes.
All inputs are finite; a program needn't handle non-finite values.
Results may differ from the reference program's by a relative error of at most 0.0003.
Values sent between devices are 32-bit elements; how exact they have to be, the bound alone decides.
No kernel may reach another device: no remote copies, remote signals or barrier semaphores. Data moves between devices by JAX's collectives and lax.ppermute only.
A program may use at most 128 MiB of HBM per device.

```python
import math
import jax
import jax.numpy as jnp
from jax import lax

BINS = 16
RADIUS = 4
X = 256
NY = 1536
NZ = 96


def draw_codes(key, part):
    base = jax.random.fold_in(key, 7)
    key_centre, key_spread, key_offset = jax.random.split(base, 3)
    block_y = NY // 8 + 1
    block_z = NZ // 8 + 1
    block_x = X // 8 + 1
    centre = jax.random.randint(key_centre, (block_y, block_z, block_x), 0, BINS)
    spread = jax.random.randint(key_spread, (block_y, block_z, block_x), 0, 4)
    index_y = jnp.arange(NY) // 8
    index_z = jnp.arange(NZ) // 8
    index_x = jnp.arange(X) // 8
    centre_cells = centre[index_y][:, index_z][:, :, index_x]
    spread_cells = spread[index_y][:, index_z][:, :, index_x]
    offset = jax.random.randint(key_offset, (NY, NZ, X), 0, 64)
    local = jnp.remainder(offset, 2 * spread_cells + 1) - spread_cells
    return jnp.remainder(centre_cells + local, BINS).astype(jnp.int32)


def level_of(own_key, extent, shards, smallest, largest):
    level = 1.0
    for axis_at, parts in shards:
        heights = jax.random.uniform(jax.random.fold_in(jax.random.fold_in(own_key, 6), axis_at), (parts,), jnp.float32, smallest / len(shards), largest / len(shards))
        level = level * jnp.repeat(jnp.exp(heights), extent[axis_at] // parts).reshape((-1,) + (1,) * (len(extent) - 1 - axis_at))
    return level


def setup_inputs(seed: int = 0) -> dict:
    splits = jax.random.split(jax.random.key(seed), 3)
    codes = draw_codes(jax.random.fold_in(splits[2], 71), 0)
    cell_volume = jnp.clip(jnp.exp(math.log(4.0) - 2.7725887 * jax.random.uniform(splits[1], (NY, NZ, X), jnp.float32) ** level_of(splits[1], (NY, NZ, X), ((0, 32), (1, 4)), -0.2, 0.2)), 0.25, 4.0)
    return dict(codes=codes, cell_volume=cell_volume)


def slide_sum(field, axis):
    widths = [(0, 0), (0, 0), (0, 0)]
    widths[axis] = (RADIUS, RADIUS)
    padded = jnp.pad(field, widths)
    length = field.shape[axis]
    total = lax.slice_in_dim(padded, 0, length, axis=axis)
    for offset in range(1, 2 * RADIUS + 1):
        total = total + lax.slice_in_dim(padded, offset, offset + length, axis=axis)
    return total


def box_sum(field):
    return slide_sum(slide_sum(slide_sum(field, 2), 0), 1)


def reference(codes, cell_volume):
    def add_bin(carry, level):
        total, spread = carry
        member = jnp.where(codes == level, cell_volume, jnp.float32(0.0))
        box = box_sum(member)
        return (total + box, spread + jax.scipy.special.xlogy(box, box)), None

    zeros = jnp.zeros(codes.shape, jnp.float32)
    (total, spread), unused = lax.scan(add_bin, (zeros, zeros), jnp.arange(BINS, dtype=jnp.int32))
    return jnp.log(total) - spread / total
```

```python
import functools
import jax
import jax.numpy as jnp
from jax import lax
from jax.experimental import pallas as pl
from jax.experimental.pallas import tpu as pltpu
from jax.sharding import PartitionSpec as P

F32, BF16, I32 = jnp.float32, jnp.bfloat16, jnp.int32
BINS, RAD, LANES = 16, 4, 128
WIN = 2 * RAD + 1
TINY = 1e-30
LN2 = 0.6931471805599453
SPLIT = True

VMEM = pl.BlockSpec(memory_space=pltpu.VMEM)
SMEM = pl.BlockSpec(memory_space=pltpu.SMEM)
ANY = pl.BlockSpec(memory_space=pl.ANY)


def params(mib):
    return pltpu.CompilerParams(vmem_limit_bytes=mib << 20)


def band(n):
    i = lax.broadcasted_iota(I32, (n, n), 0)
    j = lax.broadcasted_iota(I32, (n, n), 1)
    return jnp.where(jnp.abs(i - j) <= RAD, 1.0, 0.0).astype(BF16)


def x_sums(codes, vol, weights, store):
    rows, width = vol.shape
    code = codes.astype(BF16)
    high = vol.astype(BF16)
    parts = [high]
    if SPLIT:
        parts.append((vol - high.astype(F32)).astype(BF16))
    zero = jnp.zeros((rows, width), BF16)
    hits = [code == jnp.asarray(b, BF16) for b in range(BINS)]
    total = None
    for part in parts:
        member = jnp.concatenate([jnp.where(hit, part, zero) for hit in hits], 0)
        term = jnp.dot(member, weights, preferred_element_type=F32)
        total = term if total is None else total + term
    for b in range(BINS):
        for k in range(0, rows, 8):
            for h in range(width // LANES):
                store(b, k, h, total[rows * b + k:rows * b + k + 8, LANES * h:LANES * (h + 1)])


def pitch_store(ref, pitch):
    def store(b, k, h, value):
        ref[h, pl.ds(pitch * b + k, 8), :] = value
    return store


def pitch_load(ref, pitch, row, g, h):
    return ref[h, pl.ds(pitch * 8 * g + row, 8, stride=pitch), :]


def halo_rows(a, b):
    first = lax.broadcasted_iota(I32, a.shape, 0) < RAD
    return (jnp.where(first, a, pltpu.roll(b, RAD, 0)),
            jnp.where(first, pltpu.roll(a, RAD, 0), b))


def pack_z(codes_ref, vol_ref, par_ref, a_ref, b_ref):
    rows, nz, width = codes_ref.shape
    odd = par_ref[0]
    high = pl.multiple_of((nz - 8) * (1 - odd), 8)
    low = pl.multiple_of((nz - 8) * odd, 8)
    first = lax.broadcasted_iota(I32, (8, width), 0) < RAD

    def step(y, _):
        for start, upper, out in ((high, odd == 0, a_ref), (low, odd == 1, b_ref)):
            c = codes_ref[y, pl.ds(start, 8), :].astype(F32)
            v = vol_ref[y, pl.ds(start, 8), :]
            c2, v2 = pltpu.roll(c, RAD, 0), pltpu.roll(v, RAD, 0)
            out[y] = jnp.where(first, jnp.where(upper, c2, c), jnp.where(upper, v, v2))
        return 0
    lax.fori_loop(0, rows, step, 0, unroll=4)


def pack_y(codes_ref, vol_ref, za_ref, zb_ref, par_ref, z_ref, a_ref, b_ref):
    rows, nz, _ = codes_ref.shape
    odd = par_ref[1]
    for start, out in (((rows - RAD) * (1 - odd), a_ref), ((rows - RAD) * odd, b_ref)):
        for i in range(RAD):
            y = start + i
            out[i, 0:nz] = codes_ref[y].astype(F32)
            out[i, nz:2 * nz] = vol_ref[y]
            out[i, 2 * nz:2 * nz + 8] = za_ref[y]
            out[i, 2 * nz + 8:2 * nz + 16] = zb_ref[y]


def local_sums(codes_ref, vol_ref, z_ref, ra, rb):
    rows, nz, width = codes_ref.shape
    pitch = 2 * nz + 1
    weights = band(width)

    def matmul(k, ref):
        c = jnp.concatenate([codes_ref[2 * k], codes_ref[2 * k + 1]], 0).astype(F32)
        v = jnp.concatenate([vol_ref[2 * k], vol_ref[2 * k + 1]], 0)
        x_sums(c, v, weights, pitch_store(ref, pitch))

    def along_z(k, ref):
        for i in range(2):
            for g in range(2):
                for h in range(width // LANES):
                    w = [pitch_load(ref, pitch, nz * i + z, g, h) for z in range(nz)]
                    s = w[0]
                    for z in range(1, RAD + 1):
                        s = s + w[z]
                    for z in range(nz):
                        if z:
                            if z + RAD < nz and z > RAD:
                                s = s + (w[z + RAD] - w[z - RAD - 1])
                            elif z + RAD < nz:
                                s = s + w[z + RAD]
                            else:
                                s = s - w[z - RAD - 1]
                        z_ref[2 * k + i, z, 8 * g:8 * g + 8, LANES * h:LANES * (h + 1)] = s

    half = rows // 2
    matmul(0, ra)

    def step(j, _):
        k = 2 * j
        matmul(k + 1, rb)
        along_z(k, ra)
        matmul(jnp.minimum(k + 2, half - 1), ra)
        along_z(k + 1, rb)
        return 0
    lax.fori_loop(0, half // 2, step, 0)


def z_halo_terms(ref, pitch, base, flip, g, h):
    lo = [pitch_load(ref, pitch, base + RAD * flip + i, g, h) for i in range(RAD)]
    hi = [pitch_load(ref, pitch, base + RAD - RAD * flip + i, g, h) for i in range(RAD)]
    low, high = [lo[RAD - 1]], [hi[0]]
    for i in range(1, RAD):
        low.append(low[-1] + lo[RAD - 1 - i])
        high.append(high[-1] + hi[i])
    return low[::-1], high


def reduce_bins(ref, values):
    for z in range(8):
        ref[pl.ds(9 * z, 8), :] = values[2 * z] + values[2 * z + 1]
    terms = [ref[pl.ds(b, 8, stride=9), :] for b in range(8)]
    while len(terms) > 1:
        terms = [terms[i] + terms[i + 1] for i in range(0, len(terms), 2)]
    return terms[0]


def entropy_tile(sums, f0, f1):
    logs = [s * jnp.log2(jnp.maximum(s, TINY)) for s in sums]
    total = reduce_bins(f0, sums)
    spread = reduce_bins(f1, logs)
    return LN2 * (jnp.log2(total) - spread / total)


def tile(ref, y, zg, h):
    return [ref[y, 8 * zg + z, 8 * g:8 * g + 8, LANES * h:LANES * (h + 1)]
            for z in range(8) for g in range(2)]


def plus(a, b):
    return [p + q for p, q in zip(a, b)]


def minus(a, b):
    return [p - q for p, q in zip(a, b)]


def inner(z_in, za_ref, zb_ref, par_ref, z_ref, ent_ref, ra, rb, fold, ent, sem):
    rows, nz, _, width = z_ref.shape
    pitch = 17
    flip = 1 - par_ref[0]
    weights = band(width)

    def matmul(k, ref):
        pairs = [halo_rows(za_ref[2 * k + i], zb_ref[2 * k + i]) for i in range(2)]
        c = jnp.concatenate([p[0] for p in pairs], 0)
        v = jnp.concatenate([p[1] for p in pairs], 0)
        x_sums(c, v, weights, pitch_store(ref, pitch))

    def add(k, ref):
        for i in range(2):
            for g in range(2):
                for h in range(width // LANES):
                    low, high = z_halo_terms(ref, pitch, 8 * i, flip, g, h)
                    at = (slice(8 * g, 8 * g + 8), slice(LANES * h, LANES * (h + 1)))
                    for j in range(RAD):
                        z_ref[2 * k + i, j, *at] = z_ref[2 * k + i, j, *at] + low[j]
                        z = nz - RAD + j
                        z_ref[2 * k + i, z, *at] = z_ref[2 * k + i, z, *at] + high[j]

    half = rows // 2
    matmul(0, ra)

    def step(j, _):
        k = 2 * j
        matmul(k + 1, rb)
        add(k, ra)
        matmul(jnp.minimum(k + 2, half - 1), ra)
        add(k + 1, rb)
        return 0
    lax.fori_loop(0, half // 2, step, 0)

    for zg in range(nz // 8):
        for h in range(width // LANES):
            sums = tile(z_ref, 0, zg, h)
            for y in range(1, WIN - 1):
                sums = plus(sums, tile(z_ref, y, zg, h))

            def slide(j, sums, zg=zg, h=h):
                for i in range(2):
                    y = 2 * j + i
                    sums = plus(sums, tile(z_ref, y + WIN - 1, zg, h))
                    ent[y, 8 * zg:8 * zg + 8, LANES * h:LANES * (h + 1)] = entropy_tile(
                        sums, fold.at[2 * i], fold.at[2 * i + 1])
                    sums = minus(sums, tile(z_ref, y, zg, h))
                return sums
            lax.fori_loop(0, (rows - 2 * RAD) // 2, slide, sums)
    copy = pltpu.make_async_copy(ent, ent_ref.at[pl.ds(RAD, rows - 2 * RAD)], sem)
    copy.start()
    copy.wait()


def edges(z_ref, ya_ref, yb_ref, par_ref, ent_in, ent_ref, ra, rb, zh, fold, ent, sem):
    rows, nz, _, width = z_ref.shape
    ext = nz + 2 * RAD
    pitch = ext + 1
    flip_z, flip_y = 1 - par_ref[0], 1 - par_ref[1]
    weights = band(width)

    def matmul(src, i, ref):
        c, v = src[i, 0:nz], src[i, nz:2 * nz]
        hc, hv = halo_rows(src[i, 2 * nz:2 * nz + 8], src[i, 2 * nz + 8:2 * nz + 16])
        x_sums(jnp.concatenate([c, hc], 0), jnp.concatenate([v, hv], 0), weights, pitch_store(ref, pitch))

    def along_z(slot, ref):
        lo, hi = nz + RAD * flip_z, nz + RAD - RAD * flip_z
        order = [lo + i for i in range(RAD)] + list(range(nz)) + [hi + i for i in range(RAD)]
        for g in range(2):
            for h in range(width // LANES):
                w = [pitch_load(ref, pitch, p, g, h) for p in order]
                s = w[0]
                for z in range(1, WIN):
                    s = s + w[z]
                for z in range(nz):
                    if z:
                        s = s + (w[z + WIN - 1] - w[z - 1])
                    zh[slot, z, 8 * g:8 * g + 8, LANES * h:LANES * (h + 1)] = s

    matmul(ya_ref, 0, ra)

    def step(i, _):
        matmul(yb_ref, i, rb)
        along_z(i, ra)
        matmul(ya_ref, jnp.minimum(i + 1, RAD - 1), ra)
        along_z(RAD + i, rb)
        return 0
    lax.fori_loop(0, RAD, step, 0)

    low, high = RAD * flip_y, RAD - RAD * flip_y
    for h in range(width // LANES):
        def column(zg, _, h=h):
            z0 = pl.multiple_of(8 * zg, 8)

            def load(ref, y):
                return [ref[y, z0 + z, 8 * g:8 * g + 8, LANES * h:LANES * (h + 1)]
                        for z in range(8) for g in range(2)]
            sums = load(z_ref, 0)
            for y in range(1, RAD):
                sums = plus(sums, load(z_ref, y))
            for i in range(RAD):
                sums = plus(sums, load(zh, low + i))
            for y in range(RAD):
                sums = plus(sums, load(z_ref, y + RAD))
                ent[y, pl.ds(z0, 8), LANES * h:LANES * (h + 1)] = entropy_tile(
                    sums, fold.at[2 * (y % 2)], fold.at[2 * (y % 2) + 1])
                sums = minus(sums, load(zh, low + y))
            sums = load(z_ref, rows - 2 * RAD)
            for y in range(1, 2 * RAD):
                sums = plus(sums, load(z_ref, rows - 2 * RAD + y))
            for y in range(RAD):
                sums = plus(sums, load(zh, high + y))
                ent[RAD + y, pl.ds(z0, 8), LANES * h:LANES * (h + 1)] = entropy_tile(
                    sums, fold.at[2 * (y % 2)], fold.at[2 * (y % 2) + 1])
                sums = minus(sums, load(z_ref, rows - 2 * RAD + y))
            return 0
        lax.fori_loop(0, nz // 8, column, 0)
    copies = [pltpu.make_async_copy(ent.at[pl.ds(RAD * i, RAD)], ent_ref.at[pl.ds(y, RAD)], sem.at[i])
              for i, y in enumerate((0, rows - RAD))]
    for copy in copies:
        copy.start()
    for copy in copies:
        copy.wait()


def swaps(count, first):
    return [p for i in range(first, count - 1, 2) for p in ((i, i + 1), (i + 1, i))]


def per_device(codes, cell_volume):
    rows, nz, width = codes.shape
    count_y, count_z = lax.axis_size("gy"), lax.axis_size("gz")
    par = jnp.stack([lax.axis_index("gz") % 2, lax.axis_index("gy") % 2]).astype(I32)
    shape = jax.ShapeDtypeStruct

    za, zb = pl.pallas_call(
        pack_z, out_shape=[shape((rows, 8, width), F32)] * 2,
        in_specs=[VMEM, VMEM, SMEM], out_specs=[VMEM, VMEM],
        compiler_params=params(8), name="pack_z")(codes, cell_volume, par)
    zb = lax.ppermute(zb, "gz", swaps(count_z, 1))
    za = lax.ppermute(za, "gz", swaps(count_z, 0))

    partial = shape((rows, nz, BINS, width), F32)
    r_local = pltpu.VMEM((2, BINS * (2 * nz + 1), LANES), F32)
    z_sums = pl.pallas_call(
        local_sums, out_shape=partial, in_specs=[VMEM, VMEM], out_specs=VMEM,
        scratch_shapes=[r_local, r_local],
        compiler_params=params(16), name="local_sums")(codes, cell_volume)

    edge = shape((RAD, 2 * nz + 16, width), F32)
    ya, yb = pl.pallas_call(
        pack_y, out_shape=[edge] * 2,
        in_specs=[VMEM] * 4 + [SMEM, ANY], out_specs=[VMEM, VMEM],
        compiler_params=params(8), name="pack_y")(codes, cell_volume, za, zb, par, z_sums)
    yb = lax.ppermute(yb, "gy", swaps(count_y, 1))
    ya = lax.ppermute(ya, "gy", swaps(count_y, 0))

    fold = pltpu.VMEM((4, 72, LANES), F32)
    r_halo = pltpu.VMEM((2, BINS * 17, LANES), F32)
    z_sums, entropy = pl.pallas_call(
        inner, out_shape=[partial, shape((rows, nz, width), F32)],
        in_specs=[VMEM, VMEM, VMEM, SMEM], out_specs=[VMEM, ANY],
        scratch_shapes=[r_halo, r_halo, fold, pltpu.VMEM((rows - 2 * RAD, nz, width), F32), pltpu.SemaphoreType.DMA],
        input_output_aliases={0: 0},
        compiler_params=params(16), name="inner")(z_sums, za, zb, par)

    r_edge = pltpu.VMEM((2, BINS * (nz + 2 * RAD + 1), LANES), F32)
    return pl.pallas_call(
        edges, out_shape=shape((rows, nz, width), F32),
        in_specs=[VMEM, VMEM, VMEM, SMEM, ANY], out_specs=ANY,
        scratch_shapes=[r_edge, r_edge, pltpu.VMEM((2 * RAD, nz, BINS, width), F32), fold,
                        pltpu.VMEM((2 * RAD, nz, width), F32), pltpu.SemaphoreType.DMA((2,))],
        input_output_aliases={4: 0},
        compiler_params=params(16), name="edges")(z_sums, ya, yb, par, entropy)


def solution(mesh):
    return jax.shard_map(
        per_device,
        mesh=mesh,
        in_specs=(P("gy", "gz", None), P("gy", "gz", None)),
        out_specs=P("gy", "gz", None),
        check_vma=False,
    )
```

```python
import functools
import jax
import jax.numpy as jnp
from jax import lax
from jax.experimental import pallas as pl
from jax.experimental.pallas import tpu as pltpu
from jax.sharding import PartitionSpec as P

F32, BF16, I32 = jnp.float32, jnp.bfloat16, jnp.int32
BINS, RAD, LANES = 16, 4, 128
WIN = 2 * RAD + 1
TINY = 1e-30
LN2 = 0.6931471805599453
ACCS = 8
LOCAL, HALO, EDGE, STEPS = 4, 8, 2, 8

VMEM = pl.BlockSpec(memory_space=pltpu.VMEM)
ANY = pl.BlockSpec(memory_space=pl.ANY)
HBM = pl.BlockSpec(memory_space=pltpu.HBM)


def params(mib):
    return pltpu.CompilerParams(vmem_limit_bytes=mib << 20)


def load_weights(accs, width):
    i = lax.broadcasted_iota(I32, (width, width), 0)
    j = lax.broadcasted_iota(I32, (width, width), 1)
    weights = jnp.where(jnp.abs(i - j) <= RAD, 1.0, 0.0).astype(BF16)
    for m in range(2):
        pltpu.matmul_push_rhs(weights, 0, m)
        acc = accs[m]
        pltpu.matmul_acc_lhs(acc, jnp.zeros(acc.shape, BF16), load_staged_rhs=0)
        pltpu.matmul_pop(acc)


def with_accumulators(kernel, rows, width):
    def body(*refs):
        pl.run_scoped(lambda *accs: kernel(*refs, *accs),
                      *[pltpu.ACC(i % 2)((rows, width), F32) for i in range(ACCS)])
    return body


def x_sums(codes, vol, accs, store):
    rows, width = vol.shape
    code = codes.astype(BF16)
    high = vol.astype(BF16)
    low = (vol - high.astype(F32)).astype(BF16)
    zero = jnp.zeros((rows, width), BF16)

    def pop(b):
        total = pltpu.matmul_pop(accs[b % ACCS])
        for k in range(0, rows, 8):
            for h in range(width // LANES):
                store(b, k, h, total[k:k + 8, LANES * h:LANES * (h + 1)])

    for b in range(BINS):
        if b >= ACCS:
            pop(b - ACCS)
        hit = code == jnp.asarray(b, BF16)
        pltpu.matmul_acc_lhs(accs[b % ACCS], jnp.where(hit, high, zero))
        pltpu.matmul_acc_lhs(accs[b % ACCS], jnp.where(hit, low, zero))
    for b in range(BINS - ACCS, BINS):
        pop(b)


def pitch_store(ref, pitch):
    def store(b, k, h, value):
        ref[h, pl.ds(pitch * b + k, 8), :] = value
    return store


def pitch_load(ref, pitch, row, g, h):
    return ref[h, pl.ds(pitch * 8 * g + row, 8, stride=pitch), :]


def halo_rows(a, b):
    first = lax.broadcasted_iota(I32, a.shape, 0) < RAD
    return (jnp.where(first, a, pltpu.roll(b, RAD, 0)),
            jnp.where(first, pltpu.roll(a, RAD, 0), b))


def odd_along(axis):
    return lax.rem(lax.axis_index(axis), 2)


def pack_z(codes_ref, vol_ref, a_ref, b_ref, codes, vol, sem):
    rows, nz, width = codes_ref.shape
    odd = odd_along("gz")
    high = pl.multiple_of((nz - 8) * (1 - odd), 8)
    low = pl.multiple_of((nz - 8) * odd, 8)
    copies = []
    for i, start in enumerate((low, high)):
        for j, (src, dst) in enumerate(((codes_ref, codes), (vol_ref, vol))):
            copies.append(pltpu.make_async_copy(src.at[:, pl.ds(start, 8)], dst.at[i], sem.at[2 * i + j]))
    for copy in copies:
        copy.start()
    first = lax.broadcasted_iota(I32, (8, width), 0) < RAD

    for i, (upper, out) in enumerate(((odd == 1, b_ref), (odd == 0, a_ref))):
        copies[2 * i].wait()
        copies[2 * i + 1].wait()

        def step(y, _, i=i, upper=upper, out=out):
            c = codes[i, y].astype(F32)
            v = vol[i, y]
            c2, v2 = pltpu.roll(c, RAD, 0), pltpu.roll(v, RAD, 0)
            out[y] = jnp.where(first, jnp.where(upper, c2, c), jnp.where(upper, v, v2))
            return 0
        lax.fori_loop(0, rows, step, 0, unroll=8)


def pack_y(codes_ref, vol_ref, za_ref, zb_ref, z_ref, a_ref, b_ref):
    rows, nz, _ = codes_ref.shape
    odd = odd_along("gy")
    for start, out in (((rows - RAD) * (1 - odd), a_ref), ((rows - RAD) * odd, b_ref)):
        for i in range(RAD):
            y = start + i
            out[i, 0:nz] = codes_ref[y].astype(F32)
            out[i, nz:2 * nz] = vol_ref[y]
            out[i, 2 * nz:2 * nz + 8] = za_ref[y]
            out[i, 2 * nz + 8:2 * nz + 16] = zb_ref[y]


def stack(ref, y, n):
    return jnp.concatenate([ref[y + i] for i in range(n)], 0)


def local_sums(codes_ref, vol_ref, z_ref, ra, rb, *accs):
    rows, nz, width = codes_ref.shape
    pitch = LOCAL * nz + 1
    load_weights(accs, width)

    def matmul(k, ref):
        y = LOCAL * k
        x_sums(stack(codes_ref, y, LOCAL).astype(F32), stack(vol_ref, y, LOCAL), accs, pitch_store(ref, pitch))

    def along_z(k, ref):
        for i in range(LOCAL):
            for g in range(2):
                for h in range(width // LANES):
                    w = [pitch_load(ref, pitch, nz * i + z, g, h) for z in range(nz)]
                    s = w[0]
                    for z in range(1, RAD + 1):
                        s = s + w[z]
                    for z in range(nz):
                        if z:
                            if z + RAD < nz and z > RAD:
                                s = s + (w[z + RAD] - w[z - RAD - 1])
                            elif z + RAD < nz:
                                s = s + w[z + RAD]
                            else:
                                s = s - w[z - RAD - 1]
                        z_ref[LOCAL * k + i, z // 8, h, at_bins(z, g)] = s

    two_phase(rows // LOCAL, matmul, along_z, ra, rb)


def two_phase(count, first, second, ra, rb):
    first(0, ra)

    def step(j, _):
        first(2 * j + 1, rb)
        second(2 * j, ra)
        first(2 * j + 2, ra)
        second(2 * j + 1, rb)
        return 0
    lax.fori_loop(0, count // 2 - 1, step, 0)
    first(count - 1, rb)
    second(count - 2, ra)
    second(count - 1, rb)


def z_halo_terms(ref, pitch, base, flip, g, h):
    lo = [pitch_load(ref, pitch, base + RAD * flip + i, g, h) for i in range(RAD)]
    hi = [pitch_load(ref, pitch, base + RAD - RAD * flip + i, g, h) for i in range(RAD)]
    low, high = [lo[RAD - 1]], [hi[0]]
    for i in range(1, RAD):
        low.append(low[-1] + lo[RAD - 1 - i])
        high.append(high[-1] + hi[i])
    return low[::-1], high


def reduce_bins(ref, values):
    for z in range(8):
        ref[pl.ds(9 * z, 8), :] = values[2 * z] + values[2 * z + 1]
    terms = [ref[pl.ds(b, 8, stride=9), :] for b in range(8)]
    while len(terms) > 1:
        terms = [terms[i] + terms[i + 1] for i in range(0, len(terms), 2)]
    return terms[0]


def entropy_tile(sums, f0, f1):
    logs = [s * jnp.log2(jnp.maximum(s, TINY)) for s in sums]
    total = reduce_bins(f0, sums)
    spread = reduce_bins(f1, logs)
    return LN2 * (jnp.log2(total) - spread / total)


def tile(ref, y, zg, h):
    return [ref[y, zg, h, at_bins(z, g)] for z in range(8) for g in range(2)]


def plus(a, b):
    return [p + q for p, q in zip(a, b)]


def at_bins(z, g):
    return slice(8 * (2 * (z % 8) + g), 8 * (2 * (z % 8) + g) + 8)


def minus(a, b):
    return [p - q for p, q in zip(a, b)]


def inner(z_in, za_ref, zb_ref, z_ref, part_ref, ent_ref, ra, rb, fold, ent, sem, *accs):
    rows, nz, width = ent_ref.shape
    outs = rows - 2 * RAD
    halves = width // LANES
    pitch = 8 * HALO + 1
    flip = 1 - odd_along("gz")
    load_weights(accs, width)

    def matmul(k, ref):
        pairs = [halo_rows(za_ref[HALO * k + i], zb_ref[HALO * k + i]) for i in range(HALO)]
        c = jnp.concatenate([p[0] for p in pairs], 0)
        v = jnp.concatenate([p[1] for p in pairs], 0)
        x_sums(c, v, accs, pitch_store(ref, pitch))

    def add(k, ref):
        for i in range(HALO):
            for g in range(2):
                for h in range(halves):
                    low, high = z_halo_terms(ref, pitch, 8 * i, flip, g, h)
                    for j in range(RAD):
                        for z, term in ((j, low[j]), (nz - RAD + j, high[j])):
                            at = (HALO * k + i, z // 8, h, at_bins(z, g))
                            z_ref[at] = z_ref[at] + term

    def save(slot, zg, h, sums):
        for z in range(8):
            for g in range(2):
                part_ref[slot, zg, h, at_bins(z, g)] = sums[2 * z + g]

    def begin(zg, h):
        sums = tile(z_ref, 0, zg, h)
        for y in range(1, WIN - 1):
            sums = plus(sums, tile(z_ref, y, zg, h))
            if y >= RAD:
                save(y - RAD, zg, h, sums)
        return sums

    def slide(y, zg, h, sums, slot):
        sums = plus(sums, tile(z_ref, y + WIN - 1, zg, h))
        ent[y, 8 * zg:8 * zg + 8, LANES * h:LANES * (h + 1)] = entropy_tile(
            sums, fold.at[2 * slot], fold.at[2 * slot + 1])
        return minus(sums, tile(z_ref, y, zg, h))

    def end(zg, h, sums):
        for i in range(RAD):
            save(RAD + i, zg, h, sums)
            if i + 1 < RAD:
                sums = minus(sums, tile(z_ref, outs + i, zg, h))

    def send(zg):
        at = pl.ds(8 * zg, 8)
        return pltpu.make_async_copy(ent.at[:, at], ent_ref.at[pl.ds(RAD, outs), at], sem.at[zg])

    count, middle = rows // HALO, nz // 8 // 2
    refs = (ra, rb)
    matmul(0, ra)
    sums = [begin(middle, h) for h in range(halves)]
    for k in range(count):
        if k + 1 < count:
            matmul(k + 1, refs[(k + 1) % 2])
        add(k, refs[k % 2])
        for y in range(outs * k // count, outs * (k + 1) // count):
            for h in range(halves):
                sums[h] = slide(y, middle, h, sums[h], (2 * y + h) % STEPS)
    for h in range(halves):
        end(middle, h, sums[h])
    send(middle).start()
    for zg in range(nz // 8):
        if zg == middle:
            continue
        for h in range(halves):
            def step(j, sums, zg=zg, h=h):
                for i in range(STEPS):
                    sums = slide(STEPS * j + i, zg, h, sums, i)
                return sums
            end(zg, h, lax.fori_loop(0, outs // STEPS, step, begin(zg, h)))
        send(zg).start()
    for zg in range(nz // 8):
        send(zg).wait()


def edges(part_ref, ya_ref, yb_ref, ent_in, ent_ref, ra, rb, zh, fold, ent, sem, *accs):
    rows, nz, width = ent_ref.shape
    ext = nz + 2 * RAD
    pitch = EDGE * ext + 1
    flip_z, flip_y = 1 - odd_along("gz"), 1 - odd_along("gy")
    load_weights(accs, width)

    def matmul(src, y, ref):
        c, v = [], []
        for i in range(EDGE):
            hc, hv = halo_rows(src[y + i, 2 * nz:2 * nz + 8], src[y + i, 2 * nz + 8:2 * nz + 16])
            c += [src[y + i, 0:nz], hc]
            v += [src[y + i, nz:2 * nz], hv]
        x_sums(jnp.concatenate(c, 0), jnp.concatenate(v, 0), accs, pitch_store(ref, pitch))

    def along_z(slot, ref):
        lo, hi = nz + RAD * flip_z, nz + RAD - RAD * flip_z
        order = [lo + i for i in range(RAD)] + list(range(nz)) + [hi + i for i in range(RAD)]
        for i in range(EDGE):
            for g in range(2):
                for h in range(width // LANES):
                    w = [pitch_load(ref, pitch, ext * i + p, g, h) for p in order]
                    s = w[0]
                    for z in range(1, WIN):
                        s = s + w[z]
                    for z in range(nz):
                        if z:
                            s = s + (w[z + WIN - 1] - w[z - 1])
                        zh[slot + i, z // 8, h, at_bins(z, g)] = s

    for j in range(RAD // EDGE):
        matmul(ya_ref, EDGE * j, ra.at[j])
        matmul(yb_ref, EDGE * j, rb.at[j])
    for j in range(RAD // EDGE):
        along_z(EDGE * j, ra.at[j])
        along_z(RAD + EDGE * j, rb.at[j])

    low, high = RAD * flip_y, RAD - RAD * flip_y
    for h in range(width // LANES):
        def column(zg, _, h=h):
            z0 = pl.multiple_of(8 * zg, 8)

            def load(ref, y):
                return tile(ref, y, zg, h)

            def finish(y, sums):
                slot = 2 * (y % STEPS)
                ent[y, pl.ds(z0, 8), LANES * h:LANES * (h + 1)] = entropy_tile(
                    plus(load(part_ref, y), sums), fold.at[slot], fold.at[slot + 1])
            sums = load(zh, low + RAD - 1)
            finish(RAD - 1, sums)
            for y in range(RAD - 2, -1, -1):
                sums = plus(sums, load(zh, low + y))
                finish(y, sums)
            sums = load(zh, high)
            finish(RAD, sums)
            for y in range(1, RAD):
                sums = plus(sums, load(zh, high + y))
                finish(RAD + y, sums)
            return 0
        lax.fori_loop(0, nz // 8, column, 0)
    copies = [pltpu.make_async_copy(ent.at[pl.ds(RAD * i, RAD)], ent_ref.at[pl.ds(y, RAD)], sem.at[i])
              for i, y in enumerate((0, rows - RAD))]
    for copy in copies:
        copy.start()
    for copy in copies:
        copy.wait()


def swaps(count, first):
    return [p for i in range(first, count - 1, 2) for p in ((i, i + 1), (i + 1, i))]


def per_device(codes, cell_volume):
    rows, nz, width = codes.shape
    count_y, count_z = lax.axis_size("gy"), lax.axis_size("gz")
    shape = jax.ShapeDtypeStruct

    za, zb = pl.pallas_call(
        pack_z, out_shape=[shape((rows, 8, width), F32)] * 2,
        in_specs=[HBM, HBM], out_specs=[VMEM, VMEM],
        scratch_shapes=[pltpu.VMEM((2, rows, 8, width), I32), pltpu.VMEM((2, rows, 8, width), F32),
                        pltpu.SemaphoreType.DMA((4,))],
        compiler_params=params(8), name="pack_z")(
            pltpu.with_memory_space_constraint(codes, pltpu.HBM),
            pltpu.with_memory_space_constraint(cell_volume, pltpu.HBM))
    zb = lax.ppermute(zb, "gz", swaps(count_z, 1))
    za = lax.ppermute(za, "gz", swaps(count_z, 0))

    def sums_of(n):
        return (n, nz // 8, width // LANES, 8 * BINS, LANES)

    partial = shape(sums_of(rows), F32)
    r_local = pltpu.VMEM((2, BINS * (LOCAL * nz + 1), LANES), F32)
    z_sums = pl.pallas_call(
        with_accumulators(local_sums, LOCAL * nz, width), out_shape=partial, in_specs=[VMEM, VMEM], out_specs=VMEM,
        scratch_shapes=[r_local, r_local],
        compiler_params=params(16), name="local_sums")(codes, cell_volume)

    edge = shape((RAD, 2 * nz + 16, width), F32)
    ya, yb = pl.pallas_call(
        pack_y, out_shape=[edge] * 2,
        in_specs=[VMEM] * 4 + [ANY], out_specs=[VMEM, VMEM],
        compiler_params=params(8), name="pack_y")(codes, cell_volume, za, zb, z_sums)
    yb = lax.ppermute(yb, "gy", swaps(count_y, 1))
    ya = lax.ppermute(ya, "gy", swaps(count_y, 0))

    fold = pltpu.VMEM((2 * STEPS, 72, LANES), F32)
    r_halo = pltpu.VMEM((2, BINS * (8 * HALO + 1), LANES), F32)
    _, parts, entropy = pl.pallas_call(
        with_accumulators(inner, 8 * HALO, width), out_shape=[partial, shape(sums_of(2 * RAD), F32), shape((rows, nz, width), F32)],
        in_specs=[VMEM, VMEM, VMEM], out_specs=[VMEM, VMEM, HBM],
        scratch_shapes=[r_halo, r_halo, fold, pltpu.VMEM((rows - 2 * RAD, nz, width), F32),
                        pltpu.SemaphoreType.DMA((nz // 8,))],
        input_output_aliases={0: 0},
        compiler_params=params(16), name="inner")(z_sums, za, zb)

    r_edge = pltpu.VMEM((RAD // EDGE, 2, BINS * (EDGE * (nz + 2 * RAD) + 1), LANES), F32)
    return pl.pallas_call(
        with_accumulators(edges, EDGE * (nz + 2 * RAD), width), out_shape=shape((rows, nz, width), F32),
        in_specs=[VMEM, VMEM, VMEM, HBM], out_specs=HBM,
        scratch_shapes=[r_edge, r_edge, pltpu.VMEM(sums_of(2 * RAD), F32), fold,
                        pltpu.VMEM((2 * RAD, nz, width), F32), pltpu.SemaphoreType.DMA((2,))],
        input_output_aliases={3: 0},
        compiler_params=params(16), name="edges")(parts, ya, yb, entropy)


def solution(mesh):
    return jax.shard_map(
        per_device,
        mesh=mesh,
        in_specs=(P("gy", "gz", None), P("gy", "gz", None)),
        out_specs=P("gy", "gz", None),
        check_vma=False,
    )
```

```python
import functools
import jax
import jax.numpy as jnp
from jax import lax
from jax.experimental import pallas as pl
from jax.experimental.pallas import tpu as pltpu
from jax.sharding import PartitionSpec as P

F32, BF16, I32 = jnp.float32, jnp.bfloat16, jnp.int32
BINS, RAD, LANES = 16, 4, 128
WIN = 2 * RAD + 1
TINY = 1e-30
LN2 = 0.6931471805599453
LOCAL, HALO, EDGE, STEPS = 4, 8, 1, 8

VMEM = pl.BlockSpec(memory_space=pltpu.VMEM)
ANY = pl.BlockSpec(memory_space=pl.ANY)
HBM = pl.BlockSpec(memory_space=pltpu.HBM)


def params(mib):
    return pltpu.CompilerParams(vmem_limit_bytes=mib << 20)


def load_weights(accs, width):
    i = lax.broadcasted_iota(I32, (width, width), 0)
    j = lax.broadcasted_iota(I32, (width, width), 1)
    weights = jnp.where(jnp.abs(i - j) <= RAD, 1.0, 0.0).astype(BF16)
    for m in range(2):
        pltpu.matmul_push_rhs(weights, 0, m)
        acc = accs[m]
        pltpu.matmul_acc_lhs(acc, jnp.zeros(acc.shape, BF16), load_staged_rhs=0)
        pltpu.matmul_pop(acc)


def with_accumulators(kernel, rows, width, count):
    def body(*refs):
        pl.run_scoped(lambda *accs: kernel(*refs, *accs),
                      *[pltpu.ACC(i % 2)((rows, width), F32) for i in range(count)])
    return body


def x_sums(codes, vol, accs, store, beside=()):
    rows, width = vol.shape
    code = codes.astype(BF16)
    high = vol.astype(BF16)
    low = (vol - high.astype(F32)).astype(BF16)
    zero = jnp.zeros((rows, width), BF16)

    count = len(accs)

    def pop(b):
        total = pltpu.matmul_pop(accs[b % count])
        for k in range(0, rows, 8):
            for h in range(width // LANES):
                store(b, k, h, total[k:k + 8, LANES * h:LANES * (h + 1)])

    for b in range(BINS):
        for work in beside[len(beside) * b // BINS:len(beside) * (b + 1) // BINS]:
            work()
        if b >= count:
            pop(b - count)
        hit = code == jnp.asarray(b, BF16)
        pltpu.matmul_acc_lhs(accs[b % count], jnp.where(hit, high, zero))
        pltpu.matmul_acc_lhs(accs[b % count], jnp.where(hit, low, zero))
    for b in range(BINS - count, BINS):
        pop(b)


def pitch_store(ref, pitch):
    def store(b, k, h, value):
        ref[h, pl.ds(pitch * b + k, 8), :] = value
    return store


def pitch_load(ref, pitch, row, g, h):
    return ref[h, pl.ds(pitch * 8 * g + row, 8, stride=pitch), :]


def halo_rows(a, b):
    first = lax.broadcasted_iota(I32, a.shape, 0) < RAD
    return (jnp.where(first, a, pltpu.roll(b, RAD, 0)),
            jnp.where(first, pltpu.roll(a, RAD, 0), b))


def odd_along(axis):
    return lax.rem(lax.axis_index(axis), 2)


def pack_z(codes_ref, vol_ref, a_ref, b_ref, codes, vol, sem):
    rows, nz, width = codes_ref.shape
    odd = odd_along("gz")
    high = pl.multiple_of((nz - 8) * (1 - odd), 8)
    low = pl.multiple_of((nz - 8) * odd, 8)
    copies = []
    for i, start in enumerate((low, high)):
        for j, (src, dst) in enumerate(((codes_ref, codes), (vol_ref, vol))):
            copies.append(pltpu.make_async_copy(src.at[:, pl.ds(start, 8)], dst.at[i], sem.at[2 * i + j]))
    for copy in copies:
        copy.start()
    first = lax.broadcasted_iota(I32, (8, width), 0) < RAD

    for i, (upper, out) in enumerate(((odd == 1, b_ref), (odd == 0, a_ref))):
        copies[2 * i].wait()
        copies[2 * i + 1].wait()

        def step(y, _, i=i, upper=upper, out=out):
            c = codes[i, y].astype(F32)
            v = vol[i, y]
            c2, v2 = pltpu.roll(c, RAD, 0), pltpu.roll(v, RAD, 0)
            out[y] = jnp.where(first, jnp.where(upper, c2, c), jnp.where(upper, v, v2))
            return 0
        lax.fori_loop(0, rows, step, 0, unroll=8)


def pack_y(codes_ref, vol_ref, za_ref, zb_ref, z_ref, a_ref, b_ref):
    rows, nz, _ = codes_ref.shape
    odd = odd_along("gy")
    for start, out in (((rows - RAD) * (1 - odd), a_ref), ((rows - RAD) * odd, b_ref)):
        for i in range(RAD):
            y = start + i
            out[i, 0:nz] = codes_ref[y].astype(F32)
            out[i, nz:2 * nz] = vol_ref[y]
            out[i, 2 * nz:2 * nz + 8] = za_ref[y]
            out[i, 2 * nz + 8:2 * nz + 16] = zb_ref[y]


def stack(ref, y, n):
    return jnp.concatenate([ref[y + i] for i in range(n)], 0)


def local_sums(codes_ref, vol_ref, z_ref, ra, rb, *accs):
    rows, nz, width = codes_ref.shape
    pitch = LOCAL * nz + 1
    load_weights(accs, width)

    def matmul(k, ref, beside=()):
        y = LOCAL * k
        x_sums(stack(codes_ref, y, LOCAL).astype(F32), stack(vol_ref, y, LOCAL), accs, pitch_store(ref, pitch), beside)

    def along_z(k, ref):
        def column(i, g, h):
            w = [pitch_load(ref, pitch, nz * i + z, g, h) for z in range(nz)]
            s = w[0]
            for z in range(1, RAD + 1):
                s = s + w[z]
            for z in range(nz):
                if z:
                    if z + RAD < nz and z > RAD:
                        s = s + (w[z + RAD] - w[z - RAD - 1])
                    elif z + RAD < nz:
                        s = s + w[z + RAD]
                    else:
                        s = s - w[z - RAD - 1]
                z_ref[LOCAL * k + i, z // 8, h, at_bins(z, g)] = s
        return [functools.partial(column, i, g, h)
                for i in range(LOCAL) for g in range(2) for h in range(width // LANES)]

    count, refs = rows // LOCAL, (ra, rb)
    matmul(0, ra)
    for k in range(1, count):
        matmul(k, refs[k % 2], along_z(k - 1, refs[(k - 1) % 2]))
    for work in along_z(count - 1, refs[(count - 1) % 2]):
        work()


def two_phase(count, first, second, ra, rb):
    first(0, ra)

    def step(j, _):
        first(2 * j + 1, rb)
        second(2 * j, ra)
        first(2 * j + 2, ra)
        second(2 * j + 1, rb)
        return 0
    lax.fori_loop(0, count // 2 - 1, step, 0)
    first(count - 1, rb)
    second(count - 2, ra)
    second(count - 1, rb)


def z_halo_terms(ref, pitch, base, flip, g, h):
    lo = [pitch_load(ref, pitch, base + RAD * flip + i, g, h) for i in range(RAD)]
    hi = [pitch_load(ref, pitch, base + RAD - RAD * flip + i, g, h) for i in range(RAD)]
    low, high = [lo[RAD - 1]], [hi[0]]
    for i in range(1, RAD):
        low.append(low[-1] + lo[RAD - 1 - i])
        high.append(high[-1] + hi[i])
    return low[::-1], high


def reduce_bins(ref, values):
    for z in range(8):
        ref[pl.ds(9 * z, 8), :] = values[2 * z] + values[2 * z + 1]
    terms = [ref[pl.ds(b, 8, stride=9), :] for b in range(8)]
    while len(terms) > 1:
        terms = [terms[i] + terms[i + 1] for i in range(0, len(terms), 2)]
    return terms[0]


def entropy_tile(sums, f0, f1):
    logs = [s * jnp.log2(jnp.maximum(s, TINY)) for s in sums]
    total = reduce_bins(f0, sums)
    spread = reduce_bins(f1, logs)
    return LN2 * (jnp.log2(total) - spread / total)


def tile(ref, y, zg, h):
    return [ref[y, zg, h, at_bins(z, g)] for z in range(8) for g in range(2)]


def plus(a, b):
    return [p + q for p, q in zip(a, b)]


def at_bins(z, g):
    return slice(8 * (2 * (z % 8) + g), 8 * (2 * (z % 8) + g) + 8)


def minus(a, b):
    return [p - q for p, q in zip(a, b)]


def inner(z_in, za_ref, zb_ref, z_ref, part_ref, ent_ref, ra, rb, fold, ent, sem, *accs):
    rows, nz, width = ent_ref.shape
    outs = rows - 2 * RAD
    halves = width // LANES
    pitch = 8 * HALO + 1
    flip = 1 - odd_along("gz")
    load_weights(accs, width)

    def matmul(k, ref):
        pairs = [halo_rows(za_ref[HALO * k + i], zb_ref[HALO * k + i]) for i in range(HALO)]
        c = jnp.concatenate([p[0] for p in pairs], 0)
        v = jnp.concatenate([p[1] for p in pairs], 0)
        x_sums(c, v, accs, pitch_store(ref, pitch))

    def add(k, ref):
        for i in range(HALO):
            for g in range(2):
                for h in range(halves):
                    low, high = z_halo_terms(ref, pitch, 8 * i, flip, g, h)
                    for j in range(RAD):
                        for z, term in ((j, low[j]), (nz - RAD + j, high[j])):
                            at = (HALO * k + i, z // 8, h, at_bins(z, g))
                            z_ref[at] = z_ref[at] + term

    def save(slot, zg, h, sums):
        for z in range(8):
            for g in range(2):
                part_ref[slot, zg, h, at_bins(z, g)] = sums[2 * z + g]

    def begin(zg, h):
        sums = tile(z_ref, 0, zg, h)
        for y in range(1, WIN - 1):
            sums = plus(sums, tile(z_ref, y, zg, h))
            if y >= RAD:
                save(y - RAD, zg, h, sums)
        return sums

    def slide(y, zg, h, sums, slot):
        sums = plus(sums, tile(z_ref, y + WIN - 1, zg, h))
        ent[y, 8 * zg:8 * zg + 8, LANES * h:LANES * (h + 1)] = entropy_tile(
            sums, fold.at[2 * slot], fold.at[2 * slot + 1])
        return minus(sums, tile(z_ref, y, zg, h))

    def end(zg, h, sums):
        for i in range(RAD):
            save(RAD + i, zg, h, sums)
            if i + 1 < RAD:
                sums = minus(sums, tile(z_ref, outs + i, zg, h))

    def send(zg):
        at = pl.ds(8 * zg, 8)
        return pltpu.make_async_copy(ent.at[:, at], ent_ref.at[pl.ds(RAD, outs), at], sem.at[zg])

    count, middle = rows // HALO, nz // 8 // 2
    refs = (ra, rb)
    matmul(0, ra)
    for k in range(count):
        if k + 1 < count:
            matmul(k + 1, refs[(k + 1) % 2])
        add(k, refs[k % 2])
        h, j = divmod(k, count // halves)
        if j == 0:
            sums = begin(middle, h)
        for y in range(outs * j * halves // count, outs * (j + 1) * halves // count):
            sums = slide(y, middle, h, sums, y % STEPS)
        if (j + 1) * halves == count:
            end(middle, h, sums)
    send(middle).start()
    for zg in range(nz // 8):
        if zg == middle:
            continue
        for h in range(halves):
            def step(j, sums, zg=zg, h=h):
                for i in range(STEPS):
                    sums = slide(STEPS * j + i, zg, h, sums, i)
                return sums
            end(zg, h, lax.fori_loop(0, outs // STEPS, step, begin(zg, h)))
        send(zg).start()
    for zg in range(nz // 8):
        send(zg).wait()


def edges(part_ref, ya_ref, yb_ref, ent_in, ent_ref, ra, rb, zh, fold, ent, sem, *accs):
    rows, nz, width = ent_ref.shape
    ext = nz + 2 * RAD
    pitch = EDGE * ext + 1
    flip_z, flip_y = 1 - odd_along("gz"), 1 - odd_along("gy")
    load_weights(accs, width)

    def matmul(src, y, ref):
        c, v = [], []
        for i in range(EDGE):
            hc, hv = halo_rows(src[y + i, 2 * nz:2 * nz + 8], src[y + i, 2 * nz + 8:2 * nz + 16])
            c += [src[y + i, 0:nz], hc]
            v += [src[y + i, nz:2 * nz], hv]
        x_sums(jnp.concatenate(c, 0), jnp.concatenate(v, 0), accs, pitch_store(ref, pitch))

    def along_z(slot, ref):
        lo, hi = nz + RAD * flip_z, nz + RAD - RAD * flip_z
        order = [lo + i for i in range(RAD)] + list(range(nz)) + [hi + i for i in range(RAD)]
        for i in range(EDGE):
            for g in range(2):
                for h in range(width // LANES):
                    w = [pitch_load(ref, pitch, ext * i + p, g, h) for p in order]
                    s = w[0]
                    for z in range(1, WIN):
                        s = s + w[z]
                    for z in range(nz):
                        if z:
                            s = s + (w[z + WIN - 1] - w[z - 1])
                        zh[slot + i, z // 8, h, at_bins(z, g)] = s

    for j in range(RAD // EDGE):
        matmul(ya_ref, EDGE * j, ra.at[j])
        matmul(yb_ref, EDGE * j, rb.at[j])
    for j in range(RAD // EDGE):
        along_z(EDGE * j, ra.at[j])
        along_z(RAD + EDGE * j, rb.at[j])

    low, high = RAD * flip_y, RAD - RAD * flip_y
    for h in range(width // LANES):
        def column(zg, _, h=h):
            z0 = pl.multiple_of(8 * zg, 8)

            def load(ref, y):
                return tile(ref, y, zg, h)

            def finish(y, sums):
                slot = 2 * (y % STEPS)
                ent[y, pl.ds(z0, 8), LANES * h:LANES * (h + 1)] = entropy_tile(
                    plus(load(part_ref, y), sums), fold.at[slot], fold.at[slot + 1])
            sums = load(zh, low + RAD - 1)
            finish(RAD - 1, sums)
            for y in range(RAD - 2, -1, -1):
                sums = plus(sums, load(zh, low + y))
                finish(y, sums)
            sums = load(zh, high)
            finish(RAD, sums)
            for y in range(1, RAD):
                sums = plus(sums, load(zh, high + y))
                finish(RAD + y, sums)
            return 0
        lax.fori_loop(0, nz // 8, column, 0)
    copies = [pltpu.make_async_copy(ent.at[pl.ds(RAD * i, RAD)], ent_ref.at[pl.ds(y, RAD)], sem.at[i])
              for i, y in enumerate((0, rows - RAD))]
    for copy in copies:
        copy.start()
    for copy in copies:
        copy.wait()


def swaps(count, first):
    return [p for i in range(first, count - 1, 2) for p in ((i, i + 1), (i + 1, i))]


def per_device(codes, cell_volume):
    rows, nz, width = codes.shape
    count_y, count_z = lax.axis_size("gy"), lax.axis_size("gz")
    shape = jax.ShapeDtypeStruct

    za, zb = pl.pallas_call(
        pack_z, out_shape=[shape((rows, 8, width), F32)] * 2,
        in_specs=[HBM, HBM], out_specs=[VMEM, VMEM],
        scratch_shapes=[pltpu.VMEM((2, rows, 8, width), I32), pltpu.VMEM((2, rows, 8, width), F32),
                        pltpu.SemaphoreType.DMA((4,))],
        compiler_params=params(8), name="pack_z")(
            pltpu.with_memory_space_constraint(codes, pltpu.HBM),
            pltpu.with_memory_space_constraint(cell_volume, pltpu.HBM))
    zb = lax.ppermute(zb, "gz", swaps(count_z, 1))
    za = lax.ppermute(za, "gz", swaps(count_z, 0))

    def sums_of(n):
        return (n, nz // 8, width // LANES, 8 * BINS, LANES)

    partial = shape(sums_of(rows), F32)
    r_local = pltpu.VMEM((2, (BINS + 1) * (LOCAL * nz + 1), LANES), F32)
    z_sums = pl.pallas_call(
        with_accumulators(local_sums, LOCAL * nz, width, 8), out_shape=partial, in_specs=[VMEM, VMEM], out_specs=VMEM,
        scratch_shapes=[r_local, r_local],
        compiler_params=params(16), name="local_sums")(codes, cell_volume)

    edge = shape((RAD, 2 * nz + 16, width), F32)
    ya, yb = pl.pallas_call(
        pack_y, out_shape=[edge] * 2,
        in_specs=[VMEM] * 4 + [ANY], out_specs=[VMEM, VMEM],
        compiler_params=params(8), name="pack_y")(codes, cell_volume, za, zb, z_sums)
    yb = lax.ppermute(yb, "gy", swaps(count_y, 1))
    ya = lax.ppermute(ya, "gy", swaps(count_y, 0))

    fold = pltpu.VMEM((2 * STEPS, 80, LANES), F32)
    r_halo = pltpu.VMEM((2, (BINS + 1) * (8 * HALO + 1), LANES), F32)
    _, parts, entropy = pl.pallas_call(
        with_accumulators(inner, 8 * HALO, width, 8), out_shape=[partial, shape(sums_of(2 * RAD), F32), shape((rows, nz, width), F32)],
        in_specs=[VMEM, VMEM, VMEM], out_specs=[VMEM, VMEM, HBM],
        scratch_shapes=[r_halo, r_halo, fold, pltpu.VMEM((rows - 2 * RAD, nz, width), F32),
                        pltpu.SemaphoreType.DMA((nz // 8,))],
        input_output_aliases={0: 0},
        compiler_params=params(16), name="inner")(z_sums, za, zb)

    r_edge = pltpu.VMEM((RAD // EDGE, 2, (BINS + 1) * (EDGE * (nz + 2 * RAD) + 1), LANES), F32)
    return pl.pallas_call(
        with_accumulators(edges, EDGE * (nz + 2 * RAD), width, 16), out_shape=shape((rows, nz, width), F32),
        in_specs=[VMEM, VMEM, VMEM, HBM], out_specs=HBM,
        scratch_shapes=[r_edge, r_edge, pltpu.VMEM(sums_of(2 * RAD), F32), fold,
                        pltpu.VMEM((2 * RAD, nz, width), F32), pltpu.SemaphoreType.DMA((2,))],
        input_output_aliases={3: 0},
        compiler_params=params(16), name="edges")(parts, ya, yb, entropy)


def solution(mesh):
    return jax.shard_map(
        per_device,
        mesh=mesh,
        in_specs=(P("gy", "gz", None), P("gy", "gz", None)),
        out_specs=P("gy", "gz", None),
        check_vma=False,
    )
```

```python
import functools
import jax
import jax.numpy as jnp
from jax import lax
from jax.experimental import pallas as pl
from jax.experimental.pallas import tpu as pltpu
from jax.sharding import PartitionSpec as P

F32, BF16, I32 = jnp.float32, jnp.bfloat16, jnp.int32
BINS, RAD, LANES = 16, 4, 128
WIN = 2 * RAD + 1
TINY = 1e-30
LN2 = 0.6931471805599453
LOCAL, HALO, EDGE, STEPS = 4, 8, 1, 20

VMEM = pl.BlockSpec(memory_space=pltpu.VMEM)
ANY = pl.BlockSpec(memory_space=pl.ANY)
HBM = pl.BlockSpec(memory_space=pltpu.HBM)


def params(mib):
    return pltpu.CompilerParams(vmem_limit_bytes=mib << 20)


def load_weights(accs, width):
    i = lax.broadcasted_iota(I32, (width, width), 0)
    j = lax.broadcasted_iota(I32, (width, width), 1)
    weights = jnp.where(jnp.abs(i - j) <= RAD, 1.0, 0.0).astype(BF16)
    for m in range(2):
        pltpu.matmul_push_rhs(weights, 0, m)
        acc = accs[m]
        pltpu.matmul_acc_lhs(acc, jnp.zeros(acc.shape, BF16), load_staged_rhs=0)
        pltpu.matmul_pop(acc)


def with_accumulators(kernel, rows, width, count):
    def body(*refs):
        pl.run_scoped(lambda *accs: kernel(*refs, *accs),
                      *[pltpu.ACC(i % 2)((rows, width), F32) for i in range(count)])
    return body


def x_sums(codes, vol, accs, store, beside=()):
    rows, width = vol.shape
    code = codes.astype(BF16)
    high = vol.astype(BF16)
    low = (vol - high.astype(F32)).astype(BF16)
    zero = jnp.zeros((rows, width), BF16)

    count = len(accs)

    def pop(b):
        total = pltpu.matmul_pop(accs[b % count])
        for k in range(0, rows, 8):
            for h in range(width // LANES):
                store(b, k, h, total[k:k + 8, LANES * h:LANES * (h + 1)])

    for b in range(BINS):
        for work in beside[len(beside) * b // BINS:len(beside) * (b + 1) // BINS]:
            work()
        if b >= count:
            pop(b - count)
        hit = code == jnp.asarray(b, BF16)
        pltpu.matmul_acc_lhs(accs[b % count], jnp.where(hit, high, zero))
        pltpu.matmul_acc_lhs(accs[b % count], jnp.where(hit, low, zero))
    for b in range(BINS - count, BINS):
        pop(b)


def pitch_store(ref, pitch):
    def store(b, k, h, value):
        ref[h, pl.ds(pitch * b + k, 8), :] = value
    return store


def pitch_load(ref, pitch, row, g, h):
    return ref[h, pl.ds(pitch * 8 * g + row, 8, stride=pitch), :]


def halo_rows(a, b):
    first = lax.broadcasted_iota(I32, a.shape, 0) < RAD
    return (jnp.where(first, a, pltpu.roll(b, RAD, 0)),
            jnp.where(first, pltpu.roll(a, RAD, 0), b))


def odd_along(axis):
    return lax.rem(lax.axis_index(axis), 2)


def pack_z(codes_ref, vol_ref, a_ref, b_ref, codes, vol, sem):
    rows, nz, width = codes_ref.shape
    odd = odd_along("gz")
    high = pl.multiple_of((nz - 8) * (1 - odd), 8)
    low = pl.multiple_of((nz - 8) * odd, 8)
    copies = []
    for i, start in enumerate((low, high)):
        for j, (src, dst) in enumerate(((codes_ref, codes), (vol_ref, vol))):
            copies.append(pltpu.make_async_copy(src.at[:, pl.ds(start, 8)], dst.at[i], sem.at[2 * i + j]))
    for copy in copies:
        copy.start()
    first = lax.broadcasted_iota(I32, (8, width), 0) < RAD

    for i, (upper, out) in enumerate(((odd == 1, b_ref), (odd == 0, a_ref))):
        copies[2 * i].wait()
        copies[2 * i + 1].wait()

        def step(y, _, i=i, upper=upper, out=out):
            c = codes[i, y].astype(F32)
            v = vol[i, y]
            c2, v2 = pltpu.roll(c, RAD, 0), pltpu.roll(v, RAD, 0)
            out[y] = jnp.where(first, jnp.where(upper, c2, c), jnp.where(upper, v, v2))
            return 0
        lax.fori_loop(0, rows, step, 0, unroll=8)


def pack_y(codes_ref, vol_ref, za_ref, zb_ref, z_ref, a_ref, b_ref):
    rows, nz, _ = codes_ref.shape
    odd = odd_along("gy")
    for start, out in (((rows - RAD) * (1 - odd), a_ref), ((rows - RAD) * odd, b_ref)):
        for i in range(RAD):
            y = start + i
            out[i, 0:nz] = codes_ref[y].astype(F32)
            out[i, nz:2 * nz] = vol_ref[y]
            out[i, 2 * nz:2 * nz + 8] = za_ref[y]
            out[i, 2 * nz + 8:2 * nz + 16] = zb_ref[y]


def stack(ref, y, n):
    return jnp.concatenate([ref[y + i] for i in range(n)], 0)


def local_sums(codes_ref, vol_ref, z_ref, ra, rb, *accs):
    rows, nz, width = codes_ref.shape
    pitch = LOCAL * nz + 1
    load_weights(accs, width)

    def matmul(k, ref, beside=()):
        y = LOCAL * k
        x_sums(stack(codes_ref, y, LOCAL).astype(F32), stack(vol_ref, y, LOCAL), accs, pitch_store(ref, pitch), beside)

    def along_z(k, ref):
        def column(i, g, h):
            w = [pitch_load(ref, pitch, nz * i + z, g, h) for z in range(nz)]
            s = w[0]
            for z in range(1, RAD + 1):
                s = s + w[z]
            for z in range(nz):
                if z:
                    if z + RAD < nz and z > RAD:
                        s = s + (w[z + RAD] - w[z - RAD - 1])
                    elif z + RAD < nz:
                        s = s + w[z + RAD]
                    else:
                        s = s - w[z - RAD - 1]
                z_ref[LOCAL * k + i, z // 8, h, at_bins(z, g)] = s
        return [functools.partial(column, i, g, h)
                for i in range(LOCAL) for g in range(2) for h in range(width // LANES)]

    count, refs = rows // LOCAL, (ra, rb)
    matmul(0, ra)
    for k in range(1, count):
        matmul(k, refs[k % 2], along_z(k - 1, refs[(k - 1) % 2]))
    for work in along_z(count - 1, refs[(count - 1) % 2]):
        work()


def two_phase(count, first, second, ra, rb):
    first(0, ra)

    def step(j, _):
        first(2 * j + 1, rb)
        second(2 * j, ra)
        first(2 * j + 2, ra)
        second(2 * j + 1, rb)
        return 0
    lax.fori_loop(0, count // 2 - 1, step, 0)
    first(count - 1, rb)
    second(count - 2, ra)
    second(count - 1, rb)


def z_halo_terms(ref, pitch, base, flip, g, h):
    lo = [pitch_load(ref, pitch, base + RAD * flip + i, g, h) for i in range(RAD)]
    hi = [pitch_load(ref, pitch, base + RAD - RAD * flip + i, g, h) for i in range(RAD)]
    low, high = [lo[RAD - 1]], [hi[0]]
    for i in range(1, RAD):
        low.append(low[-1] + lo[RAD - 1 - i])
        high.append(high[-1] + hi[i])
    return low[::-1], high


def reduce_bins(ref, values):
    for z in range(8):
        ref[pl.ds(9 * z, 8), :] = values[2 * z] + values[2 * z + 1]
    terms = [ref[pl.ds(b, 8, stride=9), :] for b in range(8)]
    while len(terms) > 1:
        terms = [terms[i] + terms[i + 1] for i in range(0, len(terms), 2)]
    return terms[0]


def entropy_tile(sums, f0, f1):
    logs = [s * jnp.log2(jnp.maximum(s, TINY)) for s in sums]
    total = reduce_bins(f0, sums)
    spread = reduce_bins(f1, logs)
    return LN2 * (jnp.log2(total) - spread / total)


def tile(ref, y, zg, h):
    return [ref[y, zg, h, at_bins(z, g)] for z in range(8) for g in range(2)]


def plus(a, b):
    return [p + q for p, q in zip(a, b)]


def at_bins(z, g):
    return slice(8 * (2 * (z % 8) + g), 8 * (2 * (z % 8) + g) + 8)


def minus(a, b):
    return [p - q for p, q in zip(a, b)]


def inner(z_in, za_ref, zb_ref, z_ref, part_ref, ent_ref, ra, rb, fold, ent, sem, *accs):
    rows, nz, width = ent_ref.shape
    outs = rows - 2 * RAD
    halves = width // LANES
    pitch = 8 * HALO + 1
    flip = 1 - odd_along("gz")
    load_weights(accs, width)

    def matmul(k, ref):
        pairs = [halo_rows(za_ref[HALO * k + i], zb_ref[HALO * k + i]) for i in range(HALO)]
        c = jnp.concatenate([p[0] for p in pairs], 0)
        v = jnp.concatenate([p[1] for p in pairs], 0)
        x_sums(c, v, accs, pitch_store(ref, pitch))

    def add(k, ref):
        for i in range(HALO):
            for g in range(2):
                for h in range(halves):
                    low, high = z_halo_terms(ref, pitch, 8 * i, flip, g, h)
                    for j in range(RAD):
                        for z, term in ((j, low[j]), (nz - RAD + j, high[j])):
                            at = (HALO * k + i, z // 8, h, at_bins(z, g))
                            z_ref[at] = z_ref[at] + term

    def save(slot, zg, h, sums):
        for z in range(8):
            for g in range(2):
                part_ref[slot, zg, h, at_bins(z, g)] = sums[2 * z + g]

    def begin(zg, h):
        sums = tile(z_ref, 0, zg, h)
        for y in range(1, WIN - 1):
            sums = plus(sums, tile(z_ref, y, zg, h))
            if y >= RAD:
                save(y - RAD, zg, h, sums)
        return sums

    def slide(y, zg, h, sums, slot):
        sums = plus(sums, tile(z_ref, y + WIN - 1, zg, h))
        ent[y, 8 * zg:8 * zg + 8, LANES * h:LANES * (h + 1)] = entropy_tile(
            sums, fold.at[2 * slot], fold.at[2 * slot + 1])
        return minus(sums, tile(z_ref, y, zg, h))

    def end(zg, h, sums):
        for i in range(RAD):
            save(RAD + i, zg, h, sums)
            if i + 1 < RAD:
                sums = minus(sums, tile(z_ref, outs + i, zg, h))

    def send(zg):
        at = pl.ds(8 * zg, 8)
        return pltpu.make_async_copy(ent.at[:, at], ent_ref.at[pl.ds(RAD, outs), at], sem.at[zg])

    count, middle = rows // HALO, nz // 8 // 2
    refs = (ra, rb)
    matmul(0, ra)
    for k in range(count):
        if k + 1 < count:
            matmul(k + 1, refs[(k + 1) % 2])
        add(k, refs[k % 2])
        h, j = divmod(k, count // halves)
        if j == 0:
            sums = begin(middle, h)
        for y in range(outs * j * halves // count, outs * (j + 1) * halves // count):
            sums = slide(y, middle, h, sums, y % STEPS)
        if (j + 1) * halves == count:
            end(middle, h, sums)
    send(middle).start()
    for zg in range(nz // 8):
        if zg == middle:
            continue
        for h in range(halves):
            def step(j, sums, zg=zg, h=h):
                for i in range(STEPS):
                    sums = slide(STEPS * j + i, zg, h, sums, i)
                return sums
            end(zg, h, lax.fori_loop(0, outs // STEPS, step, begin(zg, h)))
        send(zg).start()
    for zg in range(nz // 8):
        send(zg).wait()


def edges(part_ref, ya_ref, yb_ref, ent_in, ent_ref, ra, rb, zh, fold, ent, sem, *accs):
    rows, nz, width = ent_ref.shape
    ext = nz + 2 * RAD
    pitch = EDGE * ext + 1
    flip_z, flip_y = 1 - odd_along("gz"), 1 - odd_along("gy")
    load_weights(accs, width)

    def matmul(src, y, ref):
        c, v = [], []
        for i in range(EDGE):
            hc, hv = halo_rows(src[y + i, 2 * nz:2 * nz + 8], src[y + i, 2 * nz + 8:2 * nz + 16])
            c += [src[y + i, 0:nz], hc]
            v += [src[y + i, nz:2 * nz], hv]
        x_sums(jnp.concatenate(c, 0), jnp.concatenate(v, 0), accs, pitch_store(ref, pitch))

    def along_z(slot, ref):
        lo, hi = nz + RAD * flip_z, nz + RAD - RAD * flip_z
        order = [lo + i for i in range(RAD)] + list(range(nz)) + [hi + i for i in range(RAD)]
        for i in range(EDGE):
            for g in range(2):
                for h in range(width // LANES):
                    w = [pitch_load(ref, pitch, ext * i + p, g, h) for p in order]
                    s = w[0]
                    for z in range(1, WIN):
                        s = s + w[z]
                    for z in range(nz):
                        if z:
                            s = s + (w[z + WIN - 1] - w[z - 1])
                        zh[slot + i, z // 8, h, at_bins(z, g)] = s

    for j in range(RAD // EDGE):
        matmul(ya_ref, EDGE * j, ra.at[j])
        matmul(yb_ref, EDGE * j, rb.at[j])
    for j in range(RAD // EDGE):
        along_z(EDGE * j, ra.at[j])
        along_z(RAD + EDGE * j, rb.at[j])

    low, high = RAD * flip_y, RAD - RAD * flip_y
    for h in range(width // LANES):
        def column(zg, _, h=h):
            z0 = pl.multiple_of(8 * zg, 8)

            def load(ref, y):
                return tile(ref, y, zg, h)

            def finish(y, sums):
                slot = 2 * (y % STEPS)
                ent[y, pl.ds(z0, 8), LANES * h:LANES * (h + 1)] = entropy_tile(
                    plus(load(part_ref, y), sums), fold.at[slot], fold.at[slot + 1])
            sums = load(zh, low + RAD - 1)
            finish(RAD - 1, sums)
            for y in range(RAD - 2, -1, -1):
                sums = plus(sums, load(zh, low + y))
                finish(y, sums)
            sums = load(zh, high)
            finish(RAD, sums)
            for y in range(1, RAD):
                sums = plus(sums, load(zh, high + y))
                finish(RAD + y, sums)
            return 0
        lax.fori_loop(0, nz // 8, column, 0)
    copies = [pltpu.make_async_copy(ent.at[pl.ds(RAD * i, RAD)], ent_ref.at[pl.ds(y, RAD)], sem.at[i])
              for i, y in enumerate((0, rows - RAD))]
    for copy in copies:
        copy.start()
    for copy in copies:
        copy.wait()


def swaps(count, first):
    return [p for i in range(first, count - 1, 2) for p in ((i, i + 1), (i + 1, i))]


def per_device(codes, cell_volume):
    rows, nz, width = codes.shape
    count_y, count_z = lax.axis_size("gy"), lax.axis_size("gz")
    shape = jax.ShapeDtypeStruct

    za, zb = pl.pallas_call(
        pack_z, out_shape=[shape((rows, 8, width), F32)] * 2,
        in_specs=[HBM, HBM], out_specs=[VMEM, VMEM],
        scratch_shapes=[pltpu.VMEM((2, rows, 8, width), I32), pltpu.VMEM((2, rows, 8, width), F32),
                        pltpu.SemaphoreType.DMA((4,))],
        compiler_params=params(8), name="pack_z")(
            pltpu.with_memory_space_constraint(codes, pltpu.HBM),
            pltpu.with_memory_space_constraint(cell_volume, pltpu.HBM))
    zb = lax.ppermute(zb, "gz", swaps(count_z, 1))
    za = lax.ppermute(za, "gz", swaps(count_z, 0))

    def sums_of(n):
        return (n, nz // 8, width // LANES, 8 * BINS, LANES)

    partial = shape(sums_of(rows), F32)
    r_local = pltpu.VMEM((2, (BINS + 1) * (LOCAL * nz + 1), LANES), F32)
    z_sums = pl.pallas_call(
        with_accumulators(local_sums, LOCAL * nz, width, 8), out_shape=partial, in_specs=[VMEM, VMEM], out_specs=VMEM,
        scratch_shapes=[r_local, r_local],
        compiler_params=params(16), name="local_sums")(codes, cell_volume)

    edge = shape((RAD, 2 * nz + 16, width), F32)
    ya, yb = pl.pallas_call(
        pack_y, out_shape=[edge] * 2,
        in_specs=[VMEM] * 4 + [ANY], out_specs=[VMEM, VMEM],
        compiler_params=params(8), name="pack_y")(codes, cell_volume, za, zb, z_sums)
    yb = lax.ppermute(yb, "gy", swaps(count_y, 1))
    ya = lax.ppermute(ya, "gy", swaps(count_y, 0))

    fold = pltpu.VMEM((2 * STEPS, 80, LANES), F32)
    r_halo = pltpu.VMEM((2, (BINS + 1) * (8 * HALO + 1), LANES), F32)
    _, parts, entropy = pl.pallas_call(
        with_accumulators(inner, 8 * HALO, width, 8), out_shape=[partial, shape(sums_of(2 * RAD), F32), shape((rows, nz, width), F32)],
        in_specs=[VMEM, VMEM, VMEM], out_specs=[VMEM, VMEM, HBM],
        scratch_shapes=[r_halo, r_halo, fold, pltpu.VMEM((rows - 2 * RAD, nz, width), F32),
                        pltpu.SemaphoreType.DMA((nz // 8,))],
        input_output_aliases={0: 0},
        compiler_params=params(16), name="inner")(z_sums, za, zb)

    r_edge = pltpu.VMEM((RAD // EDGE, 2, (BINS + 1) * (EDGE * (nz + 2 * RAD) + 1), LANES), F32)
    return pl.pallas_call(
        with_accumulators(edges, EDGE * (nz + 2 * RAD), width, 16), out_shape=shape((rows, nz, width), F32),
        in_specs=[VMEM, VMEM, VMEM, HBM], out_specs=HBM,
        scratch_shapes=[r_edge, r_edge, pltpu.VMEM(sums_of(2 * RAD), F32), fold,
                        pltpu.VMEM((2 * RAD, nz, width), F32), pltpu.SemaphoreType.DMA((2,))],
        input_output_aliases={3: 0},
        compiler_params=params(16), name="edges")(parts, ya, yb, entropy)


def solution(mesh):
    return jax.shard_map(
        per_device,
        mesh=mesh,
        in_specs=(P("gy", "gz", None), P("gy", "gz", None)),
        out_specs=P("gy", "gz", None),
        check_vma=False,
    )
```
